32 devices in a mesh: dx: 4 (over y, x), dy: 8 (over z, core).
Axes of the slice: x: 2, y: 2, z: 4, core: 2. Of those that a mesh axis runs over, the one named last changes fastest.
Arguments:
- fine_nodes: bfloat16 [128, 128, 512], P('dx', 'dy'), may hold values from -6 to 6
- fine_edges: bfloat16 [6, 128, 128, 512], P(None, 'dx', 'dy'), may hold values from -6 to 6
- fine_links: int32 [6, 128, 128], P(None, 'dx', 'dy'), may hold values from 0 to 48
- mid_nodes: bfloat16 [32, 32, 512], P('dx', 'dy'), may hold values from -6 to 6
- mid_edges: bfloat16 [6, 32, 32, 512], P(None, 'dx', 'dy'), may hold values from -6 to 6
- mid_links: int32 [6, 32, 32], P(None, 'dx', 'dy'), may hold values from 0 to 8
- coarse_nodes: bfloat16 [8, 8, 512], replicated, may hold values from -6 to 6
- coarse_edges: bfloat16 [6, 8, 8, 512], replicated, may hold values from -6 to 6
- coarse_links: int32 [6, 8, 8], replicated, may hold values from 0 to 63
- edge_self: bfloat16 [1, 512, 1536], replicated, may hold values from -0.25 to 0.25
- edge_sender: bfloat16 [1, 512, 1536], replicated, may hold values from -0.25 to 0.25
- edge_receiver: bfloat16 [1, 512, 1536], replicated, may hold values from -0.25 to 0.25
- edge_bias: float32 [1, 1536], replicated, may hold values from -6 to 6
- edge_output: bfloat16 [1, 1536, 512], replicated, may hold values from -0.15625 to 0.15625
- edge_gain: float32 [1, 512], replicated, may hold values from 0.1 to 1.9
- edge_shift: float32 [1, 512], replicated, may hold values from -3 to 3
- node_self: bfloat16 [1, 512, 1536], replicated, may hold values from -0.25 to 0.25
- node_summed: bfloat16 [1, 512, 1536], replicated, may hold values from -0.109375 to 0.109375
- node_bias: float32 [1, 1536], replicated, may hold values from -6 to 6
- node_output: bfloat16 [1, 1536, 512], replicated, may hold values from -0.15625 to 0.15625
- node_gain: float32 [1, 512], replicated, may hold values from 0.1 to 1.9
- node_shift: float32 [1, 512], replicated, may hold values from -3 to 3
- prolongation: bfloat16 [1, 512, 512], replicated, may hold values from -0.25 to 0.25
- pooling: bfloat16 [1, 512, 512], replicated, may hold values from -0.25 to 0.25
Outputs:
- fine_out: bfloat16 [128, 128, 512], P('dx', 'dy')
- fine_edges_out: bfloat16 [6, 128, 128, 512], P(None, 'dx', 'dy')
- mid_out: bfloat16 [32, 32, 512], P('dx', 'dy')
- mid_edges_out: bfloat16 [6, 32, 32, 512], P(None, 'dx', 'dy')
- coarse_out: bfloat16 [8, 8, 512], replicated
- coarse_edges_out: bfloat16 [6, 8, 8, 512], replicated
The draws below stay inside these ranges and needn't reach their ends.
Inputs may be any that keep to these rules, and one draw needn't show every extreme that they name: `fine_links`: code q names the sender at offset (q // 7 - 3, q % 7 - 3) from the receiver. `mid_links`: code q names the sender at offset (q // 3 - 1, q % 3 - 1) from the receiver.
All inputs are finite; a program needn't handle non-finite values.
Results may differ from the reference program's by a relative error of at most 0.012.
Values may be sent and summed in bfloat16 or wider, within the bound.
A program may use at most 128 MiB of HBM per device.

```python
import math
import jax
import jax.numpy as jnp
from jax import lax

D = 512
HIDDEN_SIZE = 1536
FANOUT = 6
FINE_REACH = 3
MID_REACH = 1
LAYERS = 1
NX = 128
NY = 128
MX = 32
MY = 32
CX = 8
CY = 8


def place_ends(values, rng, smallest, top_value):
    dims = values.shape
    index_at = [jax.random.randint(jax.random.fold_in(rng, axis), (), 0, dims[axis]) for axis in range(len(dims))]
    values = values.at[tuple(index_at)].set(smallest)
    longest = dims.index(max(dims))
    index_at[longest] = (index_at[longest] + 1) % dims[longest]
    return values.at[tuple(index_at)].set(top_value)


def level_of(stream_key, dims, pieces, least, largest):
    def one(dim, parts):
        steps = jax.random.uniform(jax.random.fold_in(jax.random.fold_in(stream_key, 6), dim), (parts,), jnp.float32, least / len(pieces), largest / len(pieces))
        return jnp.repeat(jnp.exp(steps), dims[dim] // parts).reshape((-1,) + (1,) * (len(dims) - dim - 1))

    factor_of = one(*pieces[0])
    for cut in pieces[1:]:
        factor_of = factor_of * one(*cut)
    return factor_of


def normal_values(own_key, dims, scale, bound, split=(), dtype=jnp.bfloat16):
    factor_of = level_of(own_key, dims, split, -0.22, 0.18) if split else 1.0
    entries = jax.random.normal(own_key, dims, jnp.float32) * scale * factor_of
    return jnp.minimum(jnp.maximum(entries, -bound), bound).astype(dtype)


def setup_inputs(seed: int = 0) -> dict:
    splits = jax.random.split(jax.random.key(seed), 25)
    return {
        "fine_nodes": normal_values(splits[0], (NX, NY, D), 1.0, 6.0, ((0, 4), (1, 8))),
        "fine_edges": normal_values(splits[1], (FANOUT, NX, NY, D), 1.0, 6.0, ((1, 4), (2, 8))),
        "fine_links": place_ends(jax.random.randint(splits[2], (FANOUT, NX, NY), 0, (2 * FINE_REACH + 1) ** 2), jax.random.fold_in(splits[2], 1), 0, ((2 * FINE_REACH + 1) ** 2) - 1).astype(jnp.int32),
        "mid_nodes": normal_values(splits[3], (MX, MY, D), 1.0, 6.0, ((0, 4), (1, 8))),
        "mid_edges": normal_values(splits[4], (FANOUT, MX, MY, D), 1.0, 6.0, ((1, 4), (2, 8))),
        "mid_links": place_ends(jax.random.randint(splits[5], (FANOUT, MX, MY), 0, (2 * MID_REACH + 1) ** 2), jax.random.fold_in(splits[5], 1), 0, ((2 * MID_REACH + 1) ** 2) - 1).astype(jnp.int32),
        "coarse_nodes": normal_values(splits[6], (CX, CY, D), 1.0, 6.0),
        "coarse_edges": normal_values(splits[7], (FANOUT, CX, CY, D), 1.0, 6.0),
        "coarse_links": place_ends(jax.random.randint(splits[8], (FANOUT, CX, CY), 0, CX * CY), jax.random.fold_in(splits[8], 1), 0, (CX * CY) - 1).astype(jnp.int32),
        "edge_self": normal_values(splits[9], (LAYERS, D, HIDDEN_SIZE), D ** -0.5, 0.25),
        "edge_sender": normal_values(splits[10], (LAYERS, D, HIDDEN_SIZE), D ** -0.5, 0.25),
        "edge_receiver": normal_values(splits[11], (LAYERS, D, HIDDEN_SIZE), D ** -0.5, 0.25),
        "edge_bias": normal_values(splits[12], (LAYERS, HIDDEN_SIZE), 1.0, 6.0, (), jnp.float32),
        "edge_output": normal_values(splits[13], (LAYERS, HIDDEN_SIZE, D), HIDDEN_SIZE ** -0.5, 0.15625),
        "edge_gain": jnp.clip(1.0 + 0.18 * jax.random.normal(splits[14], (LAYERS, D), jnp.float32), 0.1, 1.9),
        "edge_shift": normal_values(splits[15], (LAYERS, D), 0.5, 3.0, (), jnp.float32),
        "node_self": normal_values(splits[16], (LAYERS, D, HIDDEN_SIZE), D ** -0.5, 0.25),
        "node_summed": normal_values(splits[17], (LAYERS, D, HIDDEN_SIZE), (FANOUT * D) ** -0.5, 0.109375),
        "node_bias": normal_values(splits[18], (LAYERS, HIDDEN_SIZE), 1.0, 6.0, (), jnp.float32),
        "node_output": normal_values(splits[19], (LAYERS, HIDDEN_SIZE, D), HIDDEN_SIZE ** -0.5, 0.15625),
        "node_gain": jnp.clip(1.0 + 0.18 * jax.random.normal(splits[20], (LAYERS, D), jnp.float32), 0.1, 1.9),
        "node_shift": normal_values(splits[21], (LAYERS, D), 0.5, 3.0, (), jnp.float32),
        "prolongation": normal_values(splits[22], (LAYERS, D, D), D ** -0.5, 0.25),
        "pooling": normal_values(splits[23], (LAYERS, D, D), D ** -0.5, 0.25),
    }


epsilon = 1e-05

def normalize(values, gain_term, shift_term):
    average = lax.optimization_barrier(jnp.mean(values, axis=-1, keepdims=True))
    centred = values - average
    variance = lax.optimization_barrier(jnp.mean(centred * centred, axis=-1, keepdims=True))
    return centred * lax.rsqrt(variance + epsilon) * gain_term + shift_term

def level_update(nodes, edges, sender_terms, senders, weights):
    self_matrix, receiver_matrix, edge_bias, edge_output, edge_gain, edge_shift, node_self, node_summed, node_bias, node_output, node_gain, node_shift = weights
    fanout, height, breadth, feature = edges.shape
    places = height * breadth
    flat_nodes = nodes.reshape(places, feature)
    flat_edges = edges.reshape(fanout * places, feature)
    receiver = jnp.dot(flat_nodes, receiver_matrix, preferred_element_type=jnp.float32) + edge_bias
    latent = jnp.dot(flat_edges, self_matrix, preferred_element_type=jnp.float32).reshape(fanout, places, -1)
    latent = latent + jnp.take(sender_terms, senders.reshape(fanout, places), axis=0) + receiver[None]
    hidden = jax.nn.silu(latent).astype(jnp.bfloat16).reshape(fanout * places, -1)
    message = jnp.dot(hidden, edge_output, preferred_element_type=jnp.float32)
    new_edges = (flat_edges.astype(jnp.float32) + normalize(message, edge_gain, edge_shift)).astype(jnp.bfloat16)
    new_edges = new_edges.reshape(fanout, places, feature)
    summed = lax.optimization_barrier(jnp.sum(new_edges.astype(jnp.float32), axis=0)).astype(jnp.bfloat16)
    node_hidden = jnp.dot(flat_nodes, node_self, preferred_element_type=jnp.float32)
    node_hidden = node_hidden + jnp.dot(summed, node_summed, preferred_element_type=jnp.float32) + node_bias
    node_hidden = jax.nn.silu(node_hidden).astype(jnp.bfloat16)
    node_message = jnp.dot(node_hidden, node_output, preferred_element_type=jnp.float32)
    new_nodes = (flat_nodes.astype(jnp.float32) + normalize(node_message, node_gain, node_shift)).astype(jnp.bfloat16)
    return (new_nodes.reshape(height, breadth, feature), new_edges.reshape(fanout, height, breadth, feature))

def blocked_update(nodes, edges, sender_terms, senders, weights):
    height, breadth, feature = nodes.shape
    fanout = edges.shape[0]
    block = math.gcd(height, 8)
    groups = height // block
    node_blocks = nodes.reshape(groups, block, breadth, feature)
    edge_blocks = edges.reshape(fanout, groups, block, breadth, feature).transpose(1, 0, 2, 3, 4)
    index_blocks = senders.reshape(fanout, groups, block, breadth).transpose(1, 0, 2, 3)
    new_nodes, new_edges = lax.map(lambda block_items: level_update(block_items[0], block_items[1], sender_terms, block_items[2], weights), (node_blocks, edge_blocks, index_blocks))
    new_nodes = new_nodes.reshape(height, breadth, feature)
    new_edges = new_edges.transpose(1, 0, 2, 3, 4).reshape(fanout, height, breadth, feature)
    return (new_nodes, new_edges)

def offset_index(link_codes, reach_cells, padded_breadth):
    window_span = 2 * reach_cells + 1
    row_place = lax.broadcasted_iota(jnp.int32, link_codes.shape, 1)
    col_place = lax.broadcasted_iota(jnp.int32, link_codes.shape, 2)
    return ((row_place + link_codes // window_span) * padded_breadth + col_place + link_codes % window_span).astype(jnp.int32)

def widen(parent_values, height, breadth):
    parent_rows, parent_cols, feature = parent_values.shape
    spread_out = jnp.broadcast_to(parent_values[:, None, :, None, :], (parent_rows, 4, parent_cols, 4, feature))
    return spread_out.reshape(height, breadth, feature)

def reference(fine_nodes, fine_edges, fine_links, mid_nodes, mid_edges, mid_links, coarse_nodes, coarse_edges, coarse_links, edge_self, edge_sender, edge_receiver, edge_bias, edge_output, edge_gain, edge_shift, node_self, node_summed, node_bias, node_output, node_gain, node_shift, prolongation, pooling):
    fine_rows, fine_cols, feature = fine_nodes.shape
    mid_rows, mid_cols = (mid_nodes.shape[0], mid_nodes.shape[1])
    coarse_rows, coarse_cols = (coarse_nodes.shape[0], coarse_nodes.shape[1])
    for layer_index in range(edge_self.shape[0]):
        weights = tuple((stacked[layer_index] for stacked in (edge_self, edge_receiver, edge_bias, edge_output, edge_gain, edge_shift, node_self, node_summed, node_bias, node_output, node_gain, node_shift)))
        sender_matrix = edge_sender[layer_index]
        padded = jnp.pad(fine_nodes, ((FINE_REACH, FINE_REACH), (FINE_REACH, FINE_REACH), (0, 0)), mode='wrap')
        fine_terms = jnp.dot(padded.reshape(-1, feature), sender_matrix, preferred_element_type=jnp.float32)
        fine_index = offset_index(fine_links, FINE_REACH, fine_cols + 2 * FINE_REACH)
        fine_new, fine_edges = blocked_update(fine_nodes, fine_edges, fine_terms, fine_index, weights)
        pooled = mid_nodes.astype(jnp.float32).reshape(coarse_rows, 4, coarse_cols, 4, feature).mean(axis=(1, 3)).astype(jnp.bfloat16)
        raised = jnp.dot(pooled.reshape(-1, feature), pooling[layer_index], preferred_element_type=jnp.float32)
        coarse_nodes = (coarse_nodes.astype(jnp.float32) + raised.reshape(coarse_rows, coarse_cols, feature)).astype(jnp.bfloat16)
        coarse_terms = jnp.dot(coarse_nodes.reshape(-1, feature), sender_matrix, preferred_element_type=jnp.float32)
        coarse_nodes, coarse_edges = blocked_update(coarse_nodes, coarse_edges, coarse_terms, coarse_links, weights)
        lifted = jnp.dot(coarse_nodes.reshape(-1, feature), prolongation[layer_index], preferred_element_type=jnp.float32)
        lifted = lifted.reshape(coarse_rows, coarse_cols, feature)
        mid_nodes = (mid_nodes.astype(jnp.float32) + widen(lifted, mid_rows, mid_cols)).astype(jnp.bfloat16)
        padded = jnp.pad(mid_nodes, ((MID_REACH, MID_REACH), (MID_REACH, MID_REACH), (0, 0)), mode='wrap')
        mid_terms = jnp.dot(padded.reshape(-1, feature), sender_matrix, preferred_element_type=jnp.float32)
        mid_index = offset_index(mid_links, MID_REACH, mid_cols + 2 * MID_REACH)
        mid_nodes, mid_edges = blocked_update(mid_nodes, mid_edges, mid_terms, mid_index, weights)
        lifted_mid = jnp.dot(mid_nodes.reshape(-1, feature), prolongation[layer_index], preferred_element_type=jnp.float32)
        lifted_mid = lifted_mid.reshape(mid_rows, mid_cols, feature)
        fine_nodes = (fine_new.astype(jnp.float32) + widen(lifted_mid, fine_rows, fine_cols)).astype(jnp.bfloat16)
    return (fine_nodes, fine_edges, mid_nodes, mid_edges, coarse_nodes, coarse_edges)
```

```python
import functools

import jax
import jax.numpy as jnp
from jax import lax
from jax.experimental import pallas as pl
from jax.experimental.pallas import tpu as pltpu
from jax.sharding import PartitionSpec as P

FINE_REACH = 3
MID_REACH = 1
BLOCK = 4
epsilon = 1e-05
F32 = jnp.float32
BF16 = jnp.bfloat16


def round_up(value, unit):
    return -(-value // unit) * unit


def exchange_kernel(
    across, along, x_ref, mid_ref, pad_ref, midpad_ref, pooled_ref,
    to_left, to_right, corner_src, top, bottom, from_left, from_right, corner_dst,
    mid_rows_dst, mid_left, mid_right, mid_corner, own_pool, pools,
    near_send, near_recv, pool_send, pool_recv,
):
    rows, cols, feature = x_ref.shape
    mrows, mcols, _ = mid_ref.shape
    half = rows // 2
    reach = FINE_REACH
    total = across * along
    me_x = lax.axis_index("dx")
    me_y = lax.axis_index("dy")
    me = me_x * along + me_y
    up = lax.rem(me_x + across - 1, across)
    down = lax.rem(me_x + 1, across)
    left = lax.rem(me_y + along - 1, along)
    right = lax.rem(me_y + 1, along)

    def other(step):
        number = lax.rem(me + step, total)
        return number // along, lax.rem(number, along)

    barrier = pltpu.get_barrier_semaphore()

    def greet(step, carry):
        pl.semaphore_signal(barrier, inc=1, device_id=other(step), device_id_type=pl.DeviceIdType.MESH)
        return carry

    lax.fori_loop(1, total, greet, 0)

    mid = mid_ref[...].astype(F32)
    brows, bcols = mrows // 4, mcols // 4
    for i in range(brows):
        strip = jnp.sum(mid[4 * i : 4 * i + 4], axis=0)
        for j in range(bcols):
            own_pool[i * bcols + j : i * bcols + j + 1, :] = (
                jnp.sum(strip[4 * j : 4 * j + 4], axis=0, keepdims=True) * (1.0 / 16.0)
            ).astype(BF16).astype(F32)

    low = lax.broadcasted_iota(jnp.int32, (half, 8, feature), 1) < 4
    first_a = x_ref[0:half, 0:8].astype(F32)
    first_b = x_ref[half:rows, 0:8].astype(F32)
    to_left[...] = jnp.where(low, first_a, pltpu.roll(first_b, 4, 1)).astype(BF16)
    last_a = x_ref[0:half, cols - 8 : cols].astype(F32)
    last_b = x_ref[half:rows, cols - 8 : cols].astype(F32)
    to_right[...] = jnp.where(low, pltpu.roll(last_a, 4, 1), last_b).astype(BF16)
    corner_src[0] = x_ref[rows - reach : rows, cols - 8 : cols]
    corner_src[1] = x_ref[rows - reach : rows, 0:8]
    corner_src[2] = x_ref[0:reach, cols - 8 : cols]
    corner_src[3] = x_ref[0:reach, 0:8]

    pl.semaphore_wait(barrier, total - 1)

    def pool_copy(slot, target):
        return pltpu.make_async_remote_copy(
            src_ref=own_pool, dst_ref=pools.at[slot], send_sem=pool_send.at[slot],
            recv_sem=pool_recv.at[slot], device_id=target, device_id_type=pl.DeviceIdType.MESH,
        )

    def send_pool(step, carry):
        pool_copy(step, other(step)).start()
        return carry

    lax.fori_loop(1, total, send_pool, 0)

    plan = (
        (to_right, from_left, (me_x, right)),
        (to_left, from_right, (me_x, left)),
        (x_ref.at[pl.ds(rows - reach, reach)], top, (down, me_y)),
        (x_ref.at[pl.ds(0, reach)], bottom, (up, me_y)),
        (corner_src.at[0], corner_dst.at[0], (down, right)),
        (corner_src.at[1], corner_dst.at[1], (down, left)),
        (corner_src.at[2], corner_dst.at[2], (up, right)),
        (corner_src.at[3], corner_dst.at[3], (up, left)),
        (mid_ref, mid_left, (me_x, right)),
        (mid_ref, mid_right, (me_x, left)),
        (mid_ref.at[mrows - 1], mid_rows_dst.at[0], (down, me_y)),
        (mid_ref.at[0], mid_rows_dst.at[1], (up, me_y)),
        (mid_ref.at[mrows - 1], mid_corner.at[0], (down, right)),
        (mid_ref.at[mrows - 1], mid_corner.at[1], (down, left)),
        (mid_ref.at[0], mid_corner.at[2], (up, right)),
        (mid_ref.at[0], mid_corner.at[3], (up, left)),
    )
    copies = []
    for number, (source, target, device) in enumerate(plan):
        copy = pltpu.make_async_remote_copy(
            src_ref=source, dst_ref=target, send_sem=near_send.at[number],
            recv_sem=near_recv.at[number], device_id=device, device_id_type=pl.DeviceIdType.MESH,
        )
        copy.start()
        copies.append(copy)

    pad_ref[reach : reach + rows, 0:cols] = x_ref[...]
    pad_ref[rows + 2 * reach] = jnp.zeros((cols + 8, feature), BF16)
    midpad_ref[...] = jnp.zeros(midpad_ref.shape, F32)
    for i in range(mrows):
        midpad_ref[i * mcols : (i + 1) * mcols, :] = mid[i]

    for copy in copies:
        copy.wait()

    pad_ref[0:reach, 0:cols] = top[...]
    pad_ref[rows + reach : rows + 2 * reach, 0:cols] = bottom[...]
    fr = from_right[...].astype(F32)
    fl = from_left[...].astype(F32)
    pad_ref[reach : reach + half, cols : cols + 8] = jnp.where(low, fr, pltpu.roll(fl, 4, 1)).astype(BF16)
    pad_ref[reach + half : reach + rows, cols : cols + 8] = jnp.where(low, pltpu.roll(fr, 4, 1), fl).astype(BF16)
    low3 = lax.broadcasted_iota(jnp.int32, (reach, 8, feature), 1) < 4
    pad_ref[0:reach, cols : cols + 8] = jnp.where(
        low3, corner_dst[1].astype(F32), corner_dst[0].astype(F32)
    ).astype(BF16)
    pad_ref[rows + reach : rows + 2 * reach, cols : cols + 8] = jnp.where(
        low3, corner_dst[3].astype(F32), corner_dst[2].astype(F32)
    ).astype(BF16)

    base = mrows * mcols
    midpad_ref[base : base + mcols, :] = mid_rows_dst[0].astype(F32)
    midpad_ref[base + mcols : base + 2 * mcols, :] = mid_rows_dst[1].astype(F32)
    for side, (tile, above, below) in enumerate(((mid_left, 0, 2), (mid_right, 1, 3))):
        start = base + 2 * mcols + side * (mrows + 2) * mcols
        midpad_ref[start : start + mcols, :] = mid_corner[above].astype(F32)
        values = tile[...].astype(F32)
        for i in range(mrows):
            midpad_ref[start + (i + 1) * mcols : start + (i + 2) * mcols, :] = values[i]
        finish = start + (mrows + 1) * mcols
        midpad_ref[finish : finish + mcols, :] = mid_corner[below].astype(F32)

    def finish_pool(step, carry):
        pool_copy(step, other(step)).wait()
        return carry

    lax.fori_loop(1, total, finish_pool, 0)
    count = brows * bcols
    pooled_ref[0] = own_pool[...]
    pooled_ref[1:total] = pools[1:total]


def exchange(fine_nodes, mid_nodes):
    across, along = lax.axis_size("dx"), lax.axis_size("dy")
    rows, cols, feature = fine_nodes.shape
    mrows, mcols, _ = mid_nodes.shape
    total = across * along
    count = (mrows // 4) * (mcols // 4)
    mid_total = round_up(3 * (mrows + 2) * mcols, 128)
    vmem = pl.BlockSpec(memory_space=pltpu.VMEM)
    return pl.pallas_call(
        functools.partial(exchange_kernel, across, along),
        name="exchange",
        out_shape=(
            jax.ShapeDtypeStruct((rows + 2 * FINE_REACH + 1, cols + 8, feature), BF16),
            jax.ShapeDtypeStruct((mid_total, feature), F32),
            jax.ShapeDtypeStruct((total, count, feature), F32),
        ),
        in_specs=[vmem] * 2,
        out_specs=[vmem] * 3,
        scratch_shapes=[
            pltpu.VMEM((rows // 2, 8, feature), BF16),
            pltpu.VMEM((rows // 2, 8, feature), BF16),
            pltpu.VMEM((4, FINE_REACH, 8, feature), BF16),
            pltpu.VMEM((FINE_REACH, cols, feature), BF16),
            pltpu.VMEM((FINE_REACH, cols, feature), BF16),
            pltpu.VMEM((rows // 2, 8, feature), BF16),
            pltpu.VMEM((rows // 2, 8, feature), BF16),
            pltpu.VMEM((4, FINE_REACH, 8, feature), BF16),
            pltpu.VMEM((2, mcols, feature), BF16),
            pltpu.VMEM((mrows, mcols, feature), BF16),
            pltpu.VMEM((mrows, mcols, feature), BF16),
            pltpu.VMEM((4, mcols, feature), BF16),
            pltpu.VMEM((count, feature), F32),
            pltpu.VMEM((total, count, feature), F32),
            pltpu.SemaphoreType.DMA((16,)),
            pltpu.SemaphoreType.DMA((16,)),
            pltpu.SemaphoreType.DMA((total,)),
            pltpu.SemaphoreType.DMA((total,)),
        ],
        compiler_params=pltpu.CompilerParams(collective_id=0, has_side_effects=True),
    )(fine_nodes, mid_nodes)


def silu(values):
    half = values * 0.5
    return half + half * jnp.tanh(half)


def normalize(values, gain_term, shift_term):
    average = jnp.mean(values, axis=-1, keepdims=True)
    centred = values - average
    variance = jnp.mean(centred * centred, axis=-1, keepdims=True)
    return centred * lax.rsqrt(variance + epsilon) * gain_term + shift_term


def dot(a, b):
    return jnp.dot(a, b, preferred_element_type=F32)


def chosen(index_row, length, width):
    padded = index_row.shape[1]
    turned = jnp.transpose(jnp.broadcast_to(index_row, (128, padded)))[:length]
    lane = lax.broadcasted_iota(jnp.int32, (length, 128), 1)
    parts = [
        jnp.where(turned == lane + start, 1.0, 0.0).astype(BF16) for start in range(0, width, 128)
    ]
    return parts[0] if len(parts) == 1 else jnp.concatenate(parts, axis=1)


def update_kernel(
    fanout,
    idx_ref, idx_mid_ref, idx_coarse_ref, idx_parent_ref, idx_pool_ref,
    x_ref, e_ref, pad_ref, midpad_ref, mid_e_ref, pooled_ref, coarse_ref, coarse_e_ref,
    ws_ref, wsend_ref, wrec_ref, ebias_ref, wo_ref, egain_ref, eshift_ref,
    ns_ref, nsum_ref, nbias_ref, no_ref, ngain_ref, nshift_ref, prol_ref, pool_ref,
    x_out, e_out, mid_out, mid_e_out, coarse_out, coarse_e_out,
    terms, receivers, act, summed,
):
    step = pl.program_id(0)
    steps = pl.num_programs(0)
    hidden = ws_ref.shape[1]
    chunk = 512
    places, feature = x_ref.shape
    block = e_ref.shape[1]
    mid_places = mid_out.shape[0]
    coarse_places = coarse_ref.shape[0]

    def edge_stage(edges, pick, terms_of, receiver_of, reps):
        length = edges.shape[0]
        for start in range(0, hidden, chunk):
            cut = slice(start, start + chunk)
            z = dot(edges, ws_ref[:, cut]) + dot(pick, terms_of(cut))
            z = z.reshape(reps, length // reps, chunk) + receiver_of(cut)[None]
            act[0:length, cut] = silu(z.reshape(length, chunk)).astype(BF16)
        message = dot(act[0:length, :], wo_ref[...])
        return (edges.astype(F32) + normalize(message, egain_ref[...], eshift_ref[...])).astype(BF16)

    def total_of(new, reps):
        return jnp.sum(new.astype(F32).reshape(reps, new.shape[0] // reps, feature), axis=0).astype(BF16)

    def node_stage(nodes, incoming):
        z = dot(nodes, ns_ref[...]) + dot(incoming, nsum_ref[...]) + nbias_ref[...]
        message = dot(silu(z).astype(BF16), no_ref[...])
        return (nodes.astype(F32) + normalize(message, ngain_ref[...], nshift_ref[...])).astype(BF16)

    def small_level(nodes, sources, edges_ref, edges_out, index_ref):
        count = nodes.shape[0]
        term = dot(sources, wsend_ref[...]).astype(BF16)
        receiver = dot(nodes, wrec_ref[...]) + ebias_ref[...]
        length = fanout * count
        width = sources.shape[0]
        if length <= act.shape[0]:
            pick = chosen(index_ref[...], length, round_up(width, 128))[:, :width]
            new = edge_stage(edges_ref[...], pick, lambda cut: term[:, cut], lambda cut: receiver[:, cut], fanout)
            edges_out[...] = new
            incoming = total_of(new, fanout)
        else:
            acc = jnp.zeros((count, feature), F32)
            for k in range(fanout):
                span = slice(k * count, (k + 1) * count)
                pick = chosen(index_ref[:, span], count, round_up(width, 128))[:, :width]
                new = edge_stage(edges_ref[span, :], pick, lambda cut: term[:, cut], lambda cut: receiver[:, cut], 1)
                edges_out[span, :] = new
                acc = acc + new.astype(F32)
            incoming = acc.astype(BF16)
        return node_stage(nodes, incoming)

    @pl.when(step == 0)
    def _():
        place = chosen(idx_pool_ref[...], coarse_places, round_up(coarse_places, 128))[:, :coarse_places]
        pooled = dot(place, pooled_ref[...].astype(BF16)).astype(BF16)
        coarse_pre = (coarse_ref[...].astype(F32) + dot(pooled, pool_ref[...])).astype(BF16)
        coarse = small_level(coarse_pre, coarse_pre, coarse_e_ref, coarse_e_out, idx_coarse_ref)
        coarse_out[...] = coarse
        extent = midpad_ref.shape[0]
        pick = chosen(idx_parent_ref[...], extent, round_up(coarse_places, 128))[:, :coarse_places]
        parent = dot(pick, coarse).astype(BF16)
        mid_pre = (midpad_ref[...] + dot(parent, prol_ref[...])).astype(BF16)
        mid_out[...] = small_level(mid_pre[:mid_places], mid_pre, mid_e_ref, mid_e_out, idx_mid_ref)
        terms[...] = dot(pad_ref[...], wsend_ref[...]).astype(BF16)
        receivers[...] = dot(x_ref[...], wrec_ref[...]) + ebias_ref[...]

    window = round_up((BLOCK + 2 * FINE_REACH) * (pad_ref.shape[0] // (places // block * BLOCK + 2 * FINE_REACH + 1)), 256)
    stride = pad_ref.shape[0] // (places // block * BLOCK + 2 * FINE_REACH + 1)
    begin = pl.multiple_of(step * (BLOCK * stride), BLOCK * stride)
    here = pl.multiple_of(step * block, block)
    length = fanout * block
    pick = chosen(idx_ref[0], length, window)
    new = edge_stage(
        e_ref[...].reshape(length, feature), pick,
        lambda cut: terms[pl.ds(begin, window), cut],
        lambda cut: receivers[pl.ds(here, block), cut], fanout,
    )
    e_out[...] = new.reshape(fanout, block, feature)
    summed[pl.ds(here, block), :] = total_of(new, fanout)

    @pl.when(step == steps - 1)
    def _():
        cols = block // BLOCK
        part = 256
        for start in range(0, places, part):
            rows = slice(start, start + part)
            fresh = node_stage(x_ref[rows, :], summed[rows, :])
            number = lax.broadcasted_iota(jnp.int32, (part, mid_places), 0) + start
            lane = lax.broadcasted_iota(jnp.int32, (part, mid_places), 1)
            owner = (number // cols // 4) * (cols // 4) + (number % cols) // 4
            pick = jnp.where(owner == lane, 1.0, 0.0).astype(BF16)
            lifted = dot(dot(pick, mid_out[...]).astype(BF16), prol_ref[...])
            x_out[rows, :] = (fresh.astype(F32) + lifted).astype(BF16)


def per_device(
    fine_nodes, fine_edges, fine_links, mid_nodes, mid_edges, mid_links, coarse_nodes, coarse_edges,
    coarse_links, edge_self, edge_sender, edge_receiver, edge_bias, edge_output, edge_gain, edge_shift,
    node_self, node_summed, node_bias, node_output, node_gain, node_shift, prolongation, pooling,
):
    rows, cols, feature = fine_nodes.shape
    mrows, mcols, _ = mid_nodes.shape
    crows, ccols, _ = coarse_nodes.shape
    fanout = fine_edges.shape[0]
    across, along = lax.axis_size("dx"), lax.axis_size("dy")
    me_x, me_y = lax.axis_index("dx"), lax.axis_index("dy")
    brows, bcols = mrows // 4, mcols // 4
    places, mid_places, coarse_places = rows * cols, mrows * mcols, crows * ccols
    stride = cols + 8
    steps = rows // BLOCK
    block = BLOCK * cols
    iota = functools.partial(lax.broadcasted_iota, jnp.int32)

    pad, midpad, pooled = exchange(fine_nodes, mid_nodes)

    span = 2 * FINE_REACH + 1
    shape = fine_links.shape
    column = (iota(shape, 2) + fine_links % span + (stride - FINE_REACH)) % stride
    index = (iota(shape, 1) % BLOCK + fine_links // span) * stride + column
    index = index.reshape(fanout, steps, block).transpose(1, 0, 2).reshape(steps, 1, fanout * block)

    shape = mid_links.shape
    line = iota(shape, 1) + mid_links // 3 - 1
    column = iota(shape, 2) + mid_links % 3 - 1
    centre = jnp.where(
        line < 0, mid_places + column, jnp.where(line >= mrows, mid_places + mcols + column, line * mcols + column)
    )
    side = mid_places + 2 * mcols + (line + 1) * mcols
    mid_index = jnp.where(
        column < 0, side + mcols - 1, jnp.where(column >= mcols, side + (mrows + 2) * mcols, centre)
    ).reshape(1, fanout * mid_places)
    short = round_up(fanout * mid_places, 128) - fanout * mid_places
    mid_index = jnp.pad(mid_index, ((0, 0), (0, short)))

    extent = midpad.shape[0]
    row = iota((1, extent), 1)
    beside = row - mid_places - 2 * mcols
    deep = (mrows + 2) * mcols
    line = jnp.where(
        row < mid_places, row // mcols,
        jnp.where(row < mid_places + mcols, -1, jnp.where(beside < 0, mrows, (beside % deep) // mcols - 1)),
    )
    column = jnp.where(beside < 0, row % mcols, jnp.where(beside < deep, -1, mcols))
    line = (me_x * mrows + line + across * mrows) % (across * mrows)
    column = (me_y * mcols + column + along * mcols) % (along * mcols)
    parent_index = (line // 4) * ccols + column // 4

    wide = round_up(coarse_places, 128)
    row = iota((1, wide), 1)
    line, column = row // ccols, row % ccols
    sender = (line // brows) * along + column // bcols
    slot = (me_x * along + me_y - sender + 2 * across * along) % (across * along)
    pool_index = slot * (brows * bcols) + (line % brows) * bcols + column % bcols
    coarse_index = coarse_links.reshape(1, fanout * coarse_places)

    whole = lambda shape: pl.BlockSpec(shape, lambda i: (0,) * len(shape), pipeline_mode=pl.Buffered(1))
    operands = [
        (index, pl.BlockSpec((1, 1, fanout * block), lambda i: (i, 0, 0))),
        mid_index,
        coarse_index,
        parent_index,
        pool_index,
        fine_nodes.reshape(places, feature),
        (fine_edges.reshape(fanout, places, feature), pl.BlockSpec((fanout, block, feature), lambda i: (0, i, 0))),
        pad.reshape(-1, feature),
        midpad,
        mid_edges.reshape(fanout * mid_places, feature),
        pooled.reshape(coarse_places, feature),
        coarse_nodes.reshape(coarse_places, feature),
        coarse_edges.reshape(fanout * coarse_places, feature),
    ]
    operands += [
        stacked[0] if stacked.ndim == 3 else stacked
        for stacked in (
            edge_self, edge_sender, edge_receiver, edge_bias, edge_output, edge_gain, edge_shift,
            node_self, node_summed, node_bias, node_output, node_gain, node_shift, prolongation, pooling,
        )
    ]
    specs = [item[1] if isinstance(item, tuple) else whole(item.shape) for item in operands]
    values = [item[0] if isinstance(item, tuple) else item for item in operands]
    hidden = edge_self.shape[2]
    struct = lambda *shape: jax.ShapeDtypeStruct(shape, BF16)
    fixed = lambda shape: pl.BlockSpec(shape, lambda i: (0,) * len(shape))
    fine_out, fine_e, mid_out, mid_e, coarse_out, coarse_e = pl.pallas_call(
        functools.partial(update_kernel, fanout),
        name="update",
        grid=(steps,),
        in_specs=specs,
        out_shape=(
            struct(places, feature),
            struct(fanout, places, feature),
            struct(mid_places, feature),
            struct(fanout * mid_places, feature),
            struct(coarse_places, feature),
            struct(fanout * coarse_places, feature),
        ),
        out_specs=(
            fixed((places, feature)),
            pl.BlockSpec((fanout, block, feature), lambda i: (0, i, 0)),
            fixed((mid_places, feature)),
            fixed((fanout * mid_places, feature)),
            fixed((coarse_places, feature)),
            fixed((fanout * coarse_places, feature)),
        ),
        scratch_shapes=[
            pltpu.VMEM(((rows + 2 * FINE_REACH + 1) * stride, hidden), BF16),
            pltpu.VMEM((places, hidden), F32),
            pltpu.VMEM((fanout * block, hidden), BF16),
            pltpu.VMEM((places, feature), BF16),
        ],
        compiler_params=pltpu.CompilerParams(vmem_limit_bytes=60 * 1024 * 1024),
    )(*values)
    return (
        fine_out.reshape(fine_nodes.shape),
        fine_e.reshape(fine_edges.shape),
        mid_out.reshape(mid_nodes.shape),
        mid_e.reshape(mid_edges.shape),
        coarse_out.reshape(coarse_nodes.shape),
        coarse_e.reshape(coarse_edges.shape),
    )


def solution(mesh):
    tile = P("dx", "dy", None)
    edge_tile = P(None, "dx", "dy", None)
    link_tile = P(None, "dx", "dy")
    return jax.shard_map(
        per_device,
        mesh=mesh,
        in_specs=(tile, edge_tile, link_tile) * 2 + (P(),) * 18,
        out_specs=(tile, edge_tile, tile, edge_tile, P(), P()),
        check_vma=False,
    )
```

```python
import functools

import jax
import jax.numpy as jnp
from jax import lax
from jax.experimental import pallas as pl
from jax.experimental.pallas import tpu as pltpu
from jax.sharding import PartitionSpec as P

FINE_REACH = 3
MID_REACH = 1
BLOCK = 4
epsilon = 1e-05
F32 = jnp.float32
BF16 = jnp.bfloat16


def round_up(value, unit):
    return -(-value // unit) * unit


def exchange_kernel(
    across, along, x_ref, mid_ref, pad_ref, midpad_ref, pooled_ref,
    to_left, to_right, corner_src, top, bottom, from_left, from_right, corner_dst,
    mid_src, mid_rows_dst, mid_left, mid_right, mid_corner, own_pool, pools,
    near_send, near_recv, pool_send, pool_recv,
):
    rows, cols, feature = x_ref.shape
    mrows, mcols, _ = mid_ref.shape
    half = rows // 2
    reach = FINE_REACH
    total = across * along
    me_x = lax.axis_index("dx")
    me_y = lax.axis_index("dy")
    me = me_x * along + me_y
    up = lax.rem(me_x + across - 1, across)
    down = lax.rem(me_x + 1, across)
    left = lax.rem(me_y + along - 1, along)
    right = lax.rem(me_y + 1, along)

    def other(step):
        number = lax.rem(me + step, total)
        return number // along, lax.rem(number, along)

    barrier = pltpu.get_barrier_semaphore()

    def greet(step, carry):
        pl.semaphore_signal(barrier, inc=1, device_id=other(step), device_id_type=pl.DeviceIdType.MESH)
        return carry

    lax.fori_loop(1, total, greet, 0)

    mid = mid_ref[...].astype(F32)
    brows, bcols = mrows // 4, mcols // 4
    means = []
    for i in range(brows):
        strip = jnp.sum(mid[4 * i : 4 * i + 4], axis=0)
        for j in range(bcols):
            means.append(jnp.sum(strip[4 * j : 4 * j + 4], axis=0, keepdims=True) * (1.0 / 16.0))
    own_pool[...] = jnp.concatenate(means, axis=0).astype(BF16)
    mid_src[0] = jnp.concatenate([mid[i, mcols - 1 : mcols] for i in range(mrows)], axis=0).astype(BF16)
    mid_src[1] = jnp.concatenate([mid[i, 0:1] for i in range(mrows)], axis=0).astype(BF16)

    low = lax.broadcasted_iota(jnp.int32, (half, 8, feature), 1) < 4
    first_a = x_ref[0:half, 0:8].astype(F32)
    first_b = x_ref[half:rows, 0:8].astype(F32)
    to_left[...] = jnp.where(low, first_a, pltpu.roll(first_b, 4, 1)).astype(BF16)
    last_a = x_ref[0:half, cols - 8 : cols].astype(F32)
    last_b = x_ref[half:rows, cols - 8 : cols].astype(F32)
    to_right[...] = jnp.where(low, pltpu.roll(last_a, 4, 1), last_b).astype(BF16)
    corner_src[0] = x_ref[rows - reach : rows, cols - 8 : cols]
    corner_src[1] = x_ref[rows - reach : rows, 0:8]
    corner_src[2] = x_ref[0:reach, cols - 8 : cols]
    corner_src[3] = x_ref[0:reach, 0:8]

    pl.semaphore_wait(barrier, total - 1)

    def pool_copy(slot, target):
        return pltpu.make_async_remote_copy(
            src_ref=own_pool, dst_ref=pools.at[slot], send_sem=pool_send.at[slot],
            recv_sem=pool_recv.at[slot], device_id=target, device_id_type=pl.DeviceIdType.MESH,
        )

    def send_pool(step, carry):
        pool_copy(step, other(step)).start()
        return carry

    lax.fori_loop(1, total, send_pool, 0)

    plan = (
        (to_right, from_left, (me_x, right)),
        (to_left, from_right, (me_x, left)),
        (x_ref.at[pl.ds(rows - reach, reach)], top, (down, me_y)),
        (x_ref.at[pl.ds(0, reach)], bottom, (up, me_y)),
        (corner_src.at[0], corner_dst.at[0], (down, right)),
        (corner_src.at[1], corner_dst.at[1], (down, left)),
        (corner_src.at[2], corner_dst.at[2], (up, right)),
        (corner_src.at[3], corner_dst.at[3], (up, left)),
        (mid_src.at[0], mid_left, (me_x, right)),
        (mid_src.at[1], mid_right, (me_x, left)),
        (mid_ref.at[mrows - 1], mid_rows_dst.at[0], (down, me_y)),
        (mid_ref.at[0], mid_rows_dst.at[1], (up, me_y)),
        (mid_ref.at[mrows - 1], mid_corner.at[0], (down, right)),
        (mid_ref.at[mrows - 1], mid_corner.at[1], (down, left)),
        (mid_ref.at[0], mid_corner.at[2], (up, right)),
        (mid_ref.at[0], mid_corner.at[3], (up, left)),
    )
    copies = []
    for number, (source, target, device) in enumerate(plan):
        copy = pltpu.make_async_remote_copy(
            src_ref=source, dst_ref=target, send_sem=near_send.at[number],
            recv_sem=near_recv.at[number], device_id=device, device_id_type=pl.DeviceIdType.MESH,
        )
        copy.start()
        copies.append(copy)

    pad_ref[reach : reach + rows, 0:cols] = x_ref[...]
    pad_ref[rows + 2 * reach] = jnp.zeros((cols + 8, feature), BF16)
    midpad_ref[...] = jnp.zeros(midpad_ref.shape, F32)
    for i in range(mrows):
        midpad_ref[i * mcols : (i + 1) * mcols, :] = mid[i]

    for copy in copies:
        copy.wait()

    pad_ref[0:reach, 0:cols] = top[...]
    pad_ref[rows + reach : rows + 2 * reach, 0:cols] = bottom[...]
    fr = from_right[...].astype(F32)
    fl = from_left[...].astype(F32)
    pad_ref[reach : reach + half, cols : cols + 8] = jnp.where(low, fr, pltpu.roll(fl, 4, 1)).astype(BF16)
    pad_ref[reach + half : reach + rows, cols : cols + 8] = jnp.where(low, pltpu.roll(fr, 4, 1), fl).astype(BF16)
    low3 = lax.broadcasted_iota(jnp.int32, (reach, 8, feature), 1) < 4
    pad_ref[0:reach, cols : cols + 8] = jnp.where(
        low3, corner_dst[1].astype(F32), corner_dst[0].astype(F32)
    ).astype(BF16)
    pad_ref[rows + reach : rows + 2 * reach, cols : cols + 8] = jnp.where(
        low3, corner_dst[3].astype(F32), corner_dst[2].astype(F32)
    ).astype(BF16)

    base = mrows * mcols
    midpad_ref[base : base + mcols, :] = mid_rows_dst[0].astype(F32)
    midpad_ref[base + mcols : base + 2 * mcols, :] = mid_rows_dst[1].astype(F32)
    for side, (tile, above, below, seat) in enumerate(((mid_left, 0, 2, mcols - 1), (mid_right, 1, 3, 0))):
        start = base + 2 * mcols + side * (mrows + 2) * mcols
        midpad_ref[start : start + mcols, :] = mid_corner[above].astype(F32)
        values = tile[...].astype(F32)
        for i in range(mrows):
            place = start + (i + 1) * mcols + seat
            midpad_ref[place : place + 1, :] = values[i : i + 1]
        finish = start + (mrows + 1) * mcols
        midpad_ref[finish : finish + mcols, :] = mid_corner[below].astype(F32)

    def finish_pool(step, carry):
        pool_copy(step, other(step)).wait()
        return carry

    lax.fori_loop(1, total, finish_pool, 0)
    count = brows * bcols
    pooled_ref[0:count, :] = own_pool[...].astype(F32)
    for slot in range(1, total):
        pooled_ref[slot * count : (slot + 1) * count, :] = pools[slot].astype(F32)


def exchange(fine_nodes, mid_nodes):
    across, along = lax.axis_size("dx"), lax.axis_size("dy")
    rows, cols, feature = fine_nodes.shape
    mrows, mcols, _ = mid_nodes.shape
    total = across * along
    count = (mrows // 4) * (mcols // 4)
    mid_total = round_up(3 * (mrows + 2) * mcols, 128)
    vmem = pl.BlockSpec(memory_space=pltpu.VMEM)
    return pl.pallas_call(
        functools.partial(exchange_kernel, across, along),
        name="exchange",
        out_shape=(
            jax.ShapeDtypeStruct((rows + 2 * FINE_REACH + 1, cols + 8, feature), BF16),
            jax.ShapeDtypeStruct((mid_total, feature), F32),
            jax.ShapeDtypeStruct((total * count, feature), F32),
        ),
        in_specs=[vmem] * 2,
        out_specs=[vmem] * 3,
        scratch_shapes=[
            pltpu.VMEM((rows // 2, 8, feature), BF16),
            pltpu.VMEM((rows // 2, 8, feature), BF16),
            pltpu.VMEM((4, FINE_REACH, 8, feature), BF16),
            pltpu.VMEM((FINE_REACH, cols, feature), BF16),
            pltpu.VMEM((FINE_REACH, cols, feature), BF16),
            pltpu.VMEM((rows // 2, 8, feature), BF16),
            pltpu.VMEM((rows // 2, 8, feature), BF16),
            pltpu.VMEM((4, FINE_REACH, 8, feature), BF16),
            pltpu.VMEM((2, mrows, feature), BF16),
            pltpu.VMEM((2, mcols, feature), BF16),
            pltpu.VMEM((mrows, feature), BF16),
            pltpu.VMEM((mrows, feature), BF16),
            pltpu.VMEM((4, mcols, feature), BF16),
            pltpu.VMEM((count, feature), BF16),
            pltpu.VMEM((total, count, feature), BF16),
            pltpu.SemaphoreType.DMA((16,)),
            pltpu.SemaphoreType.DMA((16,)),
            pltpu.SemaphoreType.DMA((total,)),
            pltpu.SemaphoreType.DMA((total,)),
        ],
        compiler_params=pltpu.CompilerParams(collective_id=0, has_side_effects=True),
    )(fine_nodes, mid_nodes)


def silu(values):
    half = values * 0.5
    return half + half * jnp.tanh(half)


def normalize(values, gain_term, shift_term):
    average = jnp.mean(values, axis=-1, keepdims=True)
    centred = values - average
    variance = jnp.mean(centred * centred, axis=-1, keepdims=True)
    return centred * lax.rsqrt(variance + epsilon) * gain_term + shift_term


def dot(a, b):
    return jnp.dot(a, b, preferred_element_type=F32)


def spread(values, length):
    lines, width = values.shape
    row = lax.broadcasted_iota(jnp.int32, (length, lines), 0)
    line = lax.broadcasted_iota(jnp.int32, (length, lines), 1) * width
    owner = jnp.where((row >= line) & (row < line + width), 1.0, 0.0).astype(BF16)
    rows = dot(owner, values.astype(BF16))
    row = lax.broadcasted_iota(jnp.int32, (length, width), 0)
    lane = lax.broadcasted_iota(jnp.int32, (length, width), 1)
    return jnp.sum(jnp.where(lax.rem(row, width) == lane, rows, 0.0), axis=1, keepdims=True)


def chosen(column, width):
    lane = lax.broadcasted_iota(jnp.int32, (column.shape[0], width), 1).astype(column.dtype)
    return jnp.where(column == lane, 1.0, 0.0).astype(BF16)


def update_kernel(
    fanout, across, along,
    links_ref, mid_links_ref, coarse_links_ref,
    x_ref, e_ref, pad_ref, midpad_ref, mid_e_ref, pooled_ref, coarse_ref, coarse_e_ref,
    ws_ref, wsend_ref, wrec_ref, ebias_ref, wo_ref, egain_ref, eshift_ref,
    ns_ref, nsum_ref, nbias_ref, no_ref, ngain_ref, nshift_ref, prol_ref, pool_ref,
    x_out, e_out, mid_out, mid_e_out, coarse_out, coarse_e_out,
    terms, receivers, act, summed, codes, mid_flat, mid_new,
):
    step = pl.program_id(0)
    steps = pl.num_programs(0)
    hidden = ws_ref.shape[1]
    chunk = 512
    places, feature = x_ref.shape
    block = e_ref.shape[1]
    mrows, mcols, _ = mid_out.shape
    mid_places = mrows * mcols
    crows, ccols = coarse_links_ref.shape[0] // fanout, coarse_links_ref.shape[1]
    lines, cols = links_ref.shape[0] // fanout, links_ref.shape[1]
    stride = cols + 8
    coarse_places = coarse_ref.shape[0]

    def edge_stage(edges, pick, terms_of, receiver_of, reps):
        length = edges.shape[0]
        for start in range(0, hidden, chunk):
            cut = slice(start, start + chunk)
            z = dot(edges, ws_ref[:, cut]) + dot(pick, terms_of(cut))
            z = z.reshape(reps, length // reps, chunk) + receiver_of(cut)[None]
            act[0:length, cut] = silu(z.reshape(length, chunk)).astype(BF16)
        message = dot(act[0:length, :], wo_ref[...])
        return (edges.astype(F32) + normalize(message, egain_ref[...], eshift_ref[...])).astype(BF16)

    def total_of(new, reps):
        return jnp.sum(new.astype(F32).reshape(reps, new.shape[0] // reps, feature), axis=0).astype(BF16)

    def node_stage(nodes, incoming):
        z = dot(nodes, ns_ref[...]) + dot(incoming, nsum_ref[...]) + nbias_ref[...]
        message = dot(silu(z).astype(BF16), no_ref[...])
        return (nodes.astype(F32) + normalize(message, ngain_ref[...], nshift_ref[...])).astype(BF16)

    def small_level(nodes, sources, edges_ref, edges_out, index):
        count = nodes.shape[0]
        term = dot(sources, wsend_ref[...]).astype(BF16)
        receiver = dot(nodes, wrec_ref[...]) + ebias_ref[...]
        length = fanout * count
        width = sources.shape[0]
        if length <= act.shape[0]:
            pick = chosen(spread(index, length), width)
            new = edge_stage(edges_ref[...].astype(BF16), pick, lambda cut: term[:, cut], lambda cut: receiver[:, cut], fanout)
            edges_out[...] = new.astype(edges_out.dtype)
            incoming = total_of(new, fanout)
        else:
            acc = jnp.zeros((count, feature), F32)
            for k in range(fanout):
                span = slice(k * count, (k + 1) * count)
                part = index.shape[0] // fanout
                pick = chosen(spread(index[k * part : (k + 1) * part], count), width)
                new = edge_stage(edges_ref[span, :].astype(BF16), pick, lambda cut: term[:, cut], lambda cut: receiver[:, cut], 1)
                edges_out[span, :] = new.astype(edges_out.dtype)
                acc = acc + new.astype(F32)
            incoming = acc.astype(BF16)
        return node_stage(nodes, incoming)

    @pl.when(step == 0)
    def _():
        me_x, me_y = lax.axis_index("dx"), lax.axis_index("dy")
        brows, bcols = mrows // 4, mcols // 4
        div, rem = lax.div, lax.rem
        row = lax.broadcasted_iota(jnp.int32, (coarse_places, 1), 0)
        line, column = div(row, ccols), rem(row, ccols)
        slot = rem(me_x * along + me_y + across * along - div(line, brows) * along - div(column, bcols), across * along)
        place = chosen(slot * (brows * bcols) + rem(line, brows) * bcols + rem(column, bcols), coarse_places)
        pooled = dot(place, pooled_ref[...].astype(BF16)).astype(BF16)
        coarse_pre = (coarse_ref[...].astype(F32) + dot(pooled, pool_ref[...])).astype(BF16)
        coarse = small_level(coarse_pre, coarse_pre, coarse_e_ref, coarse_e_out, coarse_links_ref[...].astype(F32))
        coarse_out[...] = coarse

        row = lax.broadcasted_iota(jnp.int32, (midpad_ref.shape[0], 1), 0)
        beside = row - mid_places - 2 * mcols
        deep = (mrows + 2) * mcols
        seat = jnp.maximum(beside, 0)
        line = jnp.where(
            row < mid_places, div(row, mcols),
            jnp.where(row < mid_places + mcols, -1, jnp.where(beside < 0, mrows, div(rem(seat, deep), mcols) - 1)),
        )
        column = jnp.where(beside < 0, rem(row, mcols), jnp.where(beside < deep, -1, mcols))
        line = rem(me_x * mrows + line + across * mrows, across * mrows)
        column = rem(me_y * mcols + column + along * mcols, along * mcols)
        parent = dot(chosen(div(line, 4) * ccols + div(column, 4), coarse_places), coarse).astype(BF16)
        mid_pre = (midpad_ref[...] + dot(parent, prol_ref[...])).astype(BF16)

        links = mid_links_ref[...]
        line = rem(lax.broadcasted_iota(jnp.int32, links.shape, 0), mrows) + div(links, 3) - 1
        column = lax.broadcasted_iota(jnp.int32, links.shape, 1) + rem(links, 3) - 1
        centre = jnp.where(
            line < 0, mid_places + column,
            jnp.where(line >= mrows, mid_places + mcols + column, line * mcols + column),
        )
        side = mid_places + 2 * mcols + (line + 1) * mcols
        index = jnp.where(
            column < 0, side + mcols - 1, jnp.where(column >= mcols, side + (mrows + 2) * mcols, centre)
        )
        for i in range(fanout * mrows):
            mid_flat[i * mcols : (i + 1) * mcols, :] = mid_e_ref[i].astype(F32)
        fresh = small_level(mid_pre[:mid_places], mid_pre, mid_flat, mid_flat, index.astype(F32))
        for i in range(fanout * mrows):
            mid_e_out[i] = mid_flat[i * mcols : (i + 1) * mcols, :].astype(BF16)
        mid_new[...] = fresh
        fresh = fresh.astype(F32)
        for i in range(mrows):
            mid_out[i] = fresh[i * mcols : (i + 1) * mcols].astype(BF16)

        links = links_ref[...]
        span = 2 * FINE_REACH + 1
        column = lax.broadcasted_iota(jnp.int32, links.shape, 1) + rem(links, span) + (stride - FINE_REACH)
        line = rem(lax.broadcasted_iota(jnp.int32, links.shape, 0), BLOCK) + div(links, span)
        index = (line * stride + rem(column, stride)).astype(F32)
        for k in range(fanout):
            for i in range(lines // BLOCK):
                codes[i, k * BLOCK : (k + 1) * BLOCK, :] = index[k * lines + i * BLOCK : k * lines + (i + 1) * BLOCK]
        terms[...] = dot(pad_ref[...], wsend_ref[...]).astype(BF16)
        receivers[...] = dot(x_ref[...], wrec_ref[...]) + ebias_ref[...]

    window = round_up((BLOCK + 2 * FINE_REACH) * stride, 256)
    begin = pl.multiple_of(step * (BLOCK * stride), BLOCK * stride)
    here = pl.multiple_of(step * block, block)
    length = fanout * block
    pick = chosen(spread(codes[step], length), window)
    new = edge_stage(
        e_ref[...].reshape(length, feature), pick,
        lambda cut: terms[pl.ds(begin, window), cut],
        lambda cut: receivers[pl.ds(here, block), cut], fanout,
    )
    e_out[...] = new.reshape(fanout, block, feature)
    summed[pl.ds(here, block), :] = total_of(new, fanout)

    @pl.when(step == steps - 1)
    def _():
        part = 256
        for start in range(0, places, part):
            rows = slice(start, start + part)
            fresh = node_stage(x_ref[rows, :], summed[rows, :])
            number = lax.broadcasted_iota(jnp.int32, (part, mid_places), 0) + start
            lane = lax.broadcasted_iota(jnp.int32, (part, mid_places), 1)
            owner = (number // cols // 4) * (cols // 4) + (number % cols) // 4
            pick = jnp.where(owner == lane, 1.0, 0.0).astype(BF16)
            lifted = dot(dot(pick, mid_new[...]).astype(BF16), prol_ref[...])
            x_out[rows, :] = (fresh.astype(F32) + lifted).astype(BF16)


def per_device(
    fine_nodes, fine_edges, fine_links, mid_nodes, mid_edges, mid_links, coarse_nodes, coarse_edges,
    coarse_links, edge_self, edge_sender, edge_receiver, edge_bias, edge_output, edge_gain, edge_shift,
    node_self, node_summed, node_bias, node_output, node_gain, node_shift, prolongation, pooling,
):
    rows, cols, feature = fine_nodes.shape
    mrows, mcols, _ = mid_nodes.shape
    crows, ccols, _ = coarse_nodes.shape
    fanout = fine_edges.shape[0]
    across, along = lax.axis_size("dx"), lax.axis_size("dy")
    places, mid_places, coarse_places = rows * cols, mrows * mcols, crows * ccols
    stride = cols + 8
    steps = rows // BLOCK
    block = BLOCK * cols
    pad, midpad, pooled = exchange(fine_nodes, mid_nodes)

    whole = lambda shape: pl.BlockSpec(shape, lambda i: (0,) * len(shape), pipeline_mode=pl.Buffered(1))
    operands = [
        fine_links.reshape(fanout * rows, cols),
        mid_links.reshape(fanout * mrows, mcols),
        coarse_links.reshape(fanout * crows, ccols),
        fine_nodes.reshape(places, feature),
        (fine_edges.reshape(fanout, places, feature), pl.BlockSpec((fanout, block, feature), lambda i: (0, i, 0))),
        pad.reshape(-1, feature),
        midpad,
        mid_edges.reshape(fanout * mrows, mcols, feature),
        pooled,
        coarse_nodes.reshape(coarse_places, feature),
        coarse_edges.reshape(fanout * coarse_places, feature),
    ]
    operands += [
        stacked[0] if stacked.ndim == 3 else stacked
        for stacked in (
            edge_self, edge_sender, edge_receiver, edge_bias, edge_output, edge_gain, edge_shift,
            node_self, node_summed, node_bias, node_output, node_gain, node_shift, prolongation, pooling,
        )
    ]
    specs = [item[1] if isinstance(item, tuple) else whole(item.shape) for item in operands]
    values = [item[0] if isinstance(item, tuple) else item for item in operands]
    hidden = edge_self.shape[2]
    struct = lambda *shape: jax.ShapeDtypeStruct(shape, BF16)
    fixed = lambda shape: pl.BlockSpec(shape, lambda i: (0,) * len(shape))
    fine_out, fine_e, mid_out, mid_e, coarse_out, coarse_e = pl.pallas_call(
        functools.partial(update_kernel, fanout, across, along),
        name="update",
        grid=(steps,),
        in_specs=specs,
        out_shape=(
            struct(places, feature),
            struct(fanout, places, feature),
            struct(mrows, mcols, feature),
            struct(fanout * mrows, mcols, feature),
            struct(coarse_places, feature),
            struct(fanout * coarse_places, feature),
        ),
        out_specs=(
            fixed((places, feature)),
            pl.BlockSpec((fanout, block, feature), lambda i: (0, i, 0)),
            fixed((mrows, mcols, feature)),
            fixed((fanout * mrows, mcols, feature)),
            fixed((coarse_places, feature)),
            fixed((fanout * coarse_places, feature)),
        ),
        scratch_shapes=[
            pltpu.VMEM(((rows + 2 * FINE_REACH + 1) * stride, hidden), BF16),
            pltpu.VMEM((places, hidden), F32),
            pltpu.VMEM((fanout * block, hidden), BF16),
            pltpu.VMEM((places, feature), BF16),
            pltpu.VMEM((steps, fanout * BLOCK, cols), F32),
            pltpu.VMEM((fanout * mid_places, feature), F32),
            pltpu.VMEM((mid_places, feature), BF16),
        ],
        compiler_params=pltpu.CompilerParams(vmem_limit_bytes=60 * 1024 * 1024),
    )(*values)
    return (
        fine_out.reshape(fine_nodes.shape),
        fine_e.reshape(fine_edges.shape),
        mid_out.reshape(mid_nodes.shape),
        mid_e.reshape(mid_edges.shape),
        coarse_out.reshape(coarse_nodes.shape),
        coarse_e.reshape(coarse_edges.shape),
    )


def solution(mesh):
    tile = P("dx", "dy", None)
    edge_tile = P(None, "dx", "dy", None)
    link_tile = P(None, "dx", "dy")
    return jax.shard_map(
        per_device,
        mesh=mesh,
        in_specs=(tile, edge_tile, link_tile) * 2 + (P(),) * 18,
        out_specs=(tile, edge_tile, tile, edge_tile, P(), P()),
        check_vma=False,
    )
```

```python
import functools

import jax
import jax.numpy as jnp
from jax import lax
from jax.experimental import pallas as pl
from jax.experimental.pallas import tpu as pltpu
from jax.sharding import PartitionSpec as P

FINE_REACH = 3
MID_REACH = 1
BLOCK = 4
epsilon = 1e-05
F32 = jnp.float32
BF16 = jnp.bfloat16


def round_up(value, unit):
    return -(-value // unit) * unit


def exchange_kernel(
    across, along, x_ref, mid_ref, pad_ref, midpad_ref, pooled_ref,
    to_left, to_right, corner_src, top, bottom, from_left, from_right, corner_dst,
    mid_src, mid_rows_dst, mid_left, mid_right, mid_corner, own_pool, pools,
    near_send, near_recv, pool_send, pool_recv,
):
    rows, cols, feature = x_ref.shape
    mrows, mcols, _ = mid_ref.shape
    half = rows // 2
    reach = FINE_REACH
    total = across * along
    me_x = lax.axis_index("dx")
    me_y = lax.axis_index("dy")
    me = me_x * along + me_y
    up = lax.rem(me_x + across - 1, across)
    down = lax.rem(me_x + 1, across)
    left = lax.rem(me_y + along - 1, along)
    right = lax.rem(me_y + 1, along)

    def other(step):
        number = lax.rem(me + step, total)
        return number // along, lax.rem(number, along)

    barrier = pltpu.get_barrier_semaphore()

    def greet(step, carry):
        pl.semaphore_signal(barrier, inc=1, device_id=other(step), device_id_type=pl.DeviceIdType.MESH)
        return carry

    lax.fori_loop(1, total, greet, 0)

    mid = mid_ref[...].astype(F32)
    brows, bcols = mrows // 4, mcols // 4
    means = []
    for i in range(brows):
        strip = jnp.sum(mid[4 * i : 4 * i + 4], axis=0)
        for j in range(bcols):
            means.append(jnp.sum(strip[4 * j : 4 * j + 4], axis=0, keepdims=True) * (1.0 / 16.0))
    own_pool[...] = jnp.concatenate(means, axis=0).astype(BF16)
    mid_src[0] = jnp.concatenate([mid[i, mcols - 1 : mcols] for i in range(mrows)], axis=0).astype(BF16)
    mid_src[1] = jnp.concatenate([mid[i, 0:1] for i in range(mrows)], axis=0).astype(BF16)

    low = lax.broadcasted_iota(jnp.int32, (half, 8, feature), 1) < 4
    first_a = x_ref[0:half, 0:8].astype(F32)
    first_b = x_ref[half:rows, 0:8].astype(F32)
    to_left[...] = jnp.where(low, first_a, pltpu.roll(first_b, 4, 1)).astype(BF16)
    last_a = x_ref[0:half, cols - 8 : cols].astype(F32)
    last_b = x_ref[half:rows, cols - 8 : cols].astype(F32)
    to_right[...] = jnp.where(low, pltpu.roll(last_a, 4, 1), last_b).astype(BF16)
    corner_src[0] = x_ref[rows - reach : rows, cols - 8 : cols]
    corner_src[1] = x_ref[rows - reach : rows, 0:8]
    corner_src[2] = x_ref[0:reach, cols - 8 : cols]
    corner_src[3] = x_ref[0:reach, 0:8]

    pl.semaphore_wait(barrier, total - 1)

    def pool_copy(slot, target):
        return pltpu.make_async_remote_copy(
            src_ref=own_pool, dst_ref=pools.at[slot], send_sem=pool_send.at[slot],
            recv_sem=pool_recv.at[slot], device_id=target, device_id_type=pl.DeviceIdType.MESH,
        )

    def send_pool(step, carry):
        pool_copy(step, other(step)).start()
        return carry

    lax.fori_loop(1, total, send_pool, 0)

    plan = (
        (to_right, from_left, (me_x, right)),
        (to_left, from_right, (me_x, left)),
        (x_ref.at[pl.ds(rows - reach, reach)], top, (down, me_y)),
        (x_ref.at[pl.ds(0, reach)], bottom, (up, me_y)),
        (corner_src.at[0], corner_dst.at[0], (down, right)),
        (corner_src.at[1], corner_dst.at[1], (down, left)),
        (corner_src.at[2], corner_dst.at[2], (up, right)),
        (corner_src.at[3], corner_dst.at[3], (up, left)),
        (mid_src.at[0], mid_left, (me_x, right)),
        (mid_src.at[1], mid_right, (me_x, left)),
        (mid_ref.at[mrows - 1], mid_rows_dst.at[0], (down, me_y)),
        (mid_ref.at[0], mid_rows_dst.at[1], (up, me_y)),
        (mid_ref.at[mrows - 1], mid_corner.at[0], (down, right)),
        (mid_ref.at[mrows - 1], mid_corner.at[1], (down, left)),
        (mid_ref.at[0], mid_corner.at[2], (up, right)),
        (mid_ref.at[0], mid_corner.at[3], (up, left)),
    )
    copies = []
    for number, (source, target, device) in enumerate(plan):
        copy = pltpu.make_async_remote_copy(
            src_ref=source, dst_ref=target, send_sem=near_send.at[number],
            recv_sem=near_recv.at[number], device_id=device, device_id_type=pl.DeviceIdType.MESH,
        )
        copy.start()
        copies.append(copy)

    pad_ref[reach : reach + rows, 0:cols] = x_ref[...]
    pad_ref[rows + 2 * reach] = jnp.zeros((cols + 8, feature), BF16)
    midpad_ref[...] = jnp.zeros(midpad_ref.shape, F32)
    for i in range(mrows):
        midpad_ref[i * mcols : (i + 1) * mcols, :] = mid[i]

    for copy in copies:
        copy.wait()

    pad_ref[0:reach, 0:cols] = top[...]
    pad_ref[rows + reach : rows + 2 * reach, 0:cols] = bottom[...]
    fr = from_right[...].astype(F32)
    fl = from_left[...].astype(F32)
    pad_ref[reach : reach + half, cols : cols + 8] = jnp.where(low, fr, pltpu.roll(fl, 4, 1)).astype(BF16)
    pad_ref[reach + half : reach + rows, cols : cols + 8] = jnp.where(low, pltpu.roll(fr, 4, 1), fl).astype(BF16)
    low3 = lax.broadcasted_iota(jnp.int32, (reach, 8, feature), 1) < 4
    pad_ref[0:reach, cols : cols + 8] = jnp.where(
        low3, corner_dst[1].astype(F32), corner_dst[0].astype(F32)
    ).astype(BF16)
    pad_ref[rows + reach : rows + 2 * reach, cols : cols + 8] = jnp.where(
        low3, corner_dst[3].astype(F32), corner_dst[2].astype(F32)
    ).astype(BF16)

    base = mrows * mcols
    midpad_ref[base : base + mcols, :] = mid_rows_dst[0].astype(F32)
    midpad_ref[base + mcols : base + 2 * mcols, :] = mid_rows_dst[1].astype(F32)
    for side, (tile, above, below, seat) in enumerate(((mid_left, 0, 2, mcols - 1), (mid_right, 1, 3, 0))):
        start = base + 2 * mcols + side * (mrows + 2) * mcols
        midpad_ref[start : start + mcols, :] = mid_corner[above].astype(F32)
        values = tile[...].astype(F32)
        for i in range(mrows):
            place = start + (i + 1) * mcols + seat
            midpad_ref[place : place + 1, :] = values[i : i + 1]
        finish = start + (mrows + 1) * mcols
        midpad_ref[finish : finish + mcols, :] = mid_corner[below].astype(F32)

    def finish_pool(step, carry):
        pool_copy(step, other(step)).wait()
        return carry

    lax.fori_loop(1, total, finish_pool, 0)
    count = brows * bcols
    pooled_ref[0:count, :] = own_pool[...].astype(F32)
    for slot in range(1, total):
        pooled_ref[slot * count : (slot + 1) * count, :] = pools[slot].astype(F32)


def exchange(fine_nodes, mid_nodes):
    across, along = lax.axis_size("dx"), lax.axis_size("dy")
    rows, cols, feature = fine_nodes.shape
    mrows, mcols, _ = mid_nodes.shape
    total = across * along
    count = (mrows // 4) * (mcols // 4)
    mid_total = round_up(3 * (mrows + 2) * mcols, 128)
    vmem = pl.BlockSpec(memory_space=pltpu.VMEM)
    return pl.pallas_call(
        functools.partial(exchange_kernel, across, along),
        name="exchange",
        out_shape=(
            jax.ShapeDtypeStruct((rows + 2 * FINE_REACH + 1, cols + 8, feature), BF16),
            jax.ShapeDtypeStruct((mid_total, feature), F32),
            jax.ShapeDtypeStruct((total * count, feature), F32),
        ),
        in_specs=[vmem] * 2,
        out_specs=[vmem] * 3,
        scratch_shapes=[
            pltpu.VMEM((rows // 2, 8, feature), BF16),
            pltpu.VMEM((rows // 2, 8, feature), BF16),
            pltpu.VMEM((4, FINE_REACH, 8, feature), BF16),
            pltpu.VMEM((FINE_REACH, cols, feature), BF16),
            pltpu.VMEM((FINE_REACH, cols, feature), BF16),
            pltpu.VMEM((rows // 2, 8, feature), BF16),
            pltpu.VMEM((rows // 2, 8, feature), BF16),
            pltpu.VMEM((4, FINE_REACH, 8, feature), BF16),
            pltpu.VMEM((2, mrows, feature), BF16),
            pltpu.VMEM((2, mcols, feature), BF16),
            pltpu.VMEM((mrows, feature), BF16),
            pltpu.VMEM((mrows, feature), BF16),
            pltpu.VMEM((4, mcols, feature), BF16),
            pltpu.VMEM((count, feature), BF16),
            pltpu.VMEM((total, count, feature), BF16),
            pltpu.SemaphoreType.DMA((16,)),
            pltpu.SemaphoreType.DMA((16,)),
            pltpu.SemaphoreType.DMA((total,)),
            pltpu.SemaphoreType.DMA((total,)),
        ],
        cost_estimate=pl.CostEstimate(flops=15_000_000_000, bytes_accessed=50_000_000, transcendentals=0),
        compiler_params=pltpu.CompilerParams(
            collective_id=0, has_side_effects=True, vmem_limit_bytes=12 * 1024 * 1024
        ),
    )(fine_nodes, mid_nodes)


def silu(values):
    half = values * 0.5
    return half + half * jnp.tanh(half)


def normalize(values, gain_term, shift_term):
    average = jnp.mean(values, axis=-1, keepdims=True)
    centred = values - average
    variance = jnp.mean(centred * centred, axis=-1, keepdims=True)
    return centred * lax.rsqrt(variance + epsilon) * gain_term + shift_term


def dot(a, b):
    return jnp.dot(a, b, preferred_element_type=F32)


def spread(values, length):
    lines, width = values.shape
    row = lax.broadcasted_iota(jnp.int32, (length, lines), 0)
    line = lax.broadcasted_iota(jnp.int32, (length, lines), 1) * width
    owner = jnp.where((row >= line) & (row < line + width), 1.0, 0.0).astype(BF16)
    rows = dot(owner, values.astype(BF16))
    row = lax.broadcasted_iota(jnp.int32, (length, width), 0)
    lane = lax.broadcasted_iota(jnp.int32, (length, width), 1)
    return jnp.sum(jnp.where(lax.rem(row, width) == lane, rows, 0.0), axis=1, keepdims=True)


def chosen(column, width):
    lane = lax.broadcasted_iota(jnp.int32, (column.shape[0], width), 1).astype(column.dtype)
    return jnp.where(column == lane, 1.0, 0.0).astype(BF16)


def update_kernel(
    fanout, across, along,
    links_ref, mid_links_ref, coarse_links_ref,
    x_ref, e_ref, pad_ref, midpad_ref, mid_e_ref, pooled_ref, coarse_ref, coarse_e_ref,
    ws_ref, wsend_ref, wrec_ref, ebias_ref, wo_ref, egain_ref, eshift_ref,
    ns_ref, nsum_ref, nbias_ref, no_ref, ngain_ref, nshift_ref, prol_ref, pool_ref,
    x_out, e_out, mid_out, mid_e_out, coarse_out, coarse_e_out,
    terms, receivers, act, summed, codes, mid_flat, mid_new,
):
    step = pl.program_id(0)
    steps = pl.num_programs(0)
    hidden = ws_ref.shape[1]
    chunk = 512
    places, feature = x_ref.shape
    block = e_ref.shape[1]
    mrows, mcols, _ = mid_out.shape
    mid_places = mrows * mcols
    crows, ccols = coarse_links_ref.shape[0] // fanout, coarse_links_ref.shape[1]
    lines, cols = links_ref.shape[0] // fanout, links_ref.shape[1]
    stride = cols + 8
    coarse_places = coarse_ref.shape[0]

    def edge_stage(edges, pick, terms_of, receiver_of, reps):
        length = edges.shape[0]
        for start in range(0, hidden, chunk):
            cut = slice(start, start + chunk)
            z = dot(edges, ws_ref[:, cut]) + dot(pick, terms_of(cut))
            z = z.reshape(reps, length // reps, chunk) + receiver_of(cut)[None]
            act[0:length, cut] = silu(z.reshape(length, chunk)).astype(BF16)
        message = dot(act[0:length, :], wo_ref[...])
        return (edges.astype(F32) + normalize(message, egain_ref[...], eshift_ref[...])).astype(BF16)

    def total_of(new, reps):
        return jnp.sum(new.astype(F32).reshape(reps, new.shape[0] // reps, feature), axis=0).astype(BF16)

    def node_stage(nodes, incoming):
        z = dot(nodes, ns_ref[...]) + dot(incoming, nsum_ref[...]) + nbias_ref[...]
        message = dot(silu(z).astype(BF16), no_ref[...])
        return (nodes.astype(F32) + normalize(message, ngain_ref[...], nshift_ref[...])).astype(BF16)

    def small_level(nodes, sources, edges_ref, edges_out, index):
        count = nodes.shape[0]
        term = dot(sources, wsend_ref[...]).astype(BF16)
        receiver = dot(nodes, wrec_ref[...]) + ebias_ref[...]
        length = fanout * count
        width = sources.shape[0]
        if length <= act.shape[0]:
            pick = chosen(spread(index, length), width)
            new = edge_stage(edges_ref[...].astype(BF16), pick, lambda cut: term[:, cut], lambda cut: receiver[:, cut], fanout)
            edges_out[...] = new.astype(edges_out.dtype)
            incoming = total_of(new, fanout)
        else:
            acc = jnp.zeros((count, feature), F32)
            for k in range(fanout):
                span = slice(k * count, (k + 1) * count)
                part = index.shape[0] // fanout
                pick = chosen(spread(index[k * part : (k + 1) * part], count), width)
                new = edge_stage(edges_ref[span, :].astype(BF16), pick, lambda cut: term[:, cut], lambda cut: receiver[:, cut], 1)
                edges_out[span, :] = new.astype(edges_out.dtype)
                acc = acc + new.astype(F32)
            incoming = acc.astype(BF16)
        return node_stage(nodes, incoming)

    @pl.when(step == 0)
    def _():
        me_x, me_y = lax.axis_index("dx"), lax.axis_index("dy")
        brows, bcols = mrows // 4, mcols // 4
        div, rem = lax.div, lax.rem
        row = lax.broadcasted_iota(jnp.int32, (coarse_places, 1), 0)
        line, column = div(row, ccols), rem(row, ccols)
        slot = rem(me_x * along + me_y + across * along - div(line, brows) * along - div(column, bcols), across * along)
        place = chosen(slot * (brows * bcols) + rem(line, brows) * bcols + rem(column, bcols), coarse_places)
        pooled = dot(place, pooled_ref[...].astype(BF16)).astype(BF16)
        coarse_pre = (coarse_ref[...].astype(F32) + dot(pooled, pool_ref[...])).astype(BF16)
        coarse = small_level(coarse_pre, coarse_pre, coarse_e_ref, coarse_e_out, coarse_links_ref[...].astype(F32))
        coarse_out[...] = coarse

        row = lax.broadcasted_iota(jnp.int32, (midpad_ref.shape[0], 1), 0)
        beside = row - mid_places - 2 * mcols
        deep = (mrows + 2) * mcols
        seat = jnp.maximum(beside, 0)
        line = jnp.where(
            row < mid_places, div(row, mcols),
            jnp.where(row < mid_places + mcols, -1, jnp.where(beside < 0, mrows, div(rem(seat, deep), mcols) - 1)),
        )
        column = jnp.where(beside < 0, rem(row, mcols), jnp.where(beside < deep, -1, mcols))
        line = rem(me_x * mrows + line + across * mrows, across * mrows)
        column = rem(me_y * mcols + column + along * mcols, along * mcols)
        parent = dot(chosen(div(line, 4) * ccols + div(column, 4), coarse_places), coarse).astype(BF16)
        mid_pre = (midpad_ref[...] + dot(parent, prol_ref[...])).astype(BF16)

        links = mid_links_ref[...]
        line = rem(lax.broadcasted_iota(jnp.int32, links.shape, 0), mrows) + div(links, 3) - 1
        column = lax.broadcasted_iota(jnp.int32, links.shape, 1) + rem(links, 3) - 1
        centre = jnp.where(
            line < 0, mid_places + column,
            jnp.where(line >= mrows, mid_places + mcols + column, line * mcols + column),
        )
        side = mid_places + 2 * mcols + (line + 1) * mcols
        index = jnp.where(
            column < 0, side + mcols - 1, jnp.where(column >= mcols, side + (mrows + 2) * mcols, centre)
        )
        for i in range(fanout * mrows):
            mid_flat[i * mcols : (i + 1) * mcols, :] = mid_e_ref[i].astype(F32)
        fresh = small_level(mid_pre[:mid_places], mid_pre, mid_flat, mid_flat, index.astype(F32))
        for i in range(fanout * mrows):
            mid_e_out[i] = mid_flat[i * mcols : (i + 1) * mcols, :].astype(BF16)
        mid_new[...] = fresh
        fresh = fresh.astype(F32)
        for i in range(mrows):
            mid_out[i] = fresh[i * mcols : (i + 1) * mcols].astype(BF16)

        links = links_ref[...]
        span = 2 * FINE_REACH + 1
        column = lax.broadcasted_iota(jnp.int32, links.shape, 1) + rem(links, span) + (stride - FINE_REACH)
        line = rem(lax.broadcasted_iota(jnp.int32, links.shape, 0), BLOCK) + div(links, span)
        index = (line * stride + rem(column, stride)).astype(F32)
        for k in range(fanout):
            for i in range(lines // BLOCK):
                codes[i, k * BLOCK : (k + 1) * BLOCK, :] = index[k * lines + i * BLOCK : k * lines + (i + 1) * BLOCK]
        terms[...] = dot(pad_ref[...], wsend_ref[...]).astype(BF16)
        receivers[...] = dot(x_ref[...], wrec_ref[...]) + ebias_ref[...]

    window = round_up((BLOCK + 2 * FINE_REACH) * stride, 256)
    begin = pl.multiple_of(step * (BLOCK * stride), BLOCK * stride)
    here = pl.multiple_of(step * block, block)
    length = fanout * block
    pick = chosen(spread(codes[step], length), window)
    new = edge_stage(
        e_ref[...].reshape(length, feature), pick,
        lambda cut: terms[pl.ds(begin, window), cut],
        lambda cut: receivers[pl.ds(here, block), cut], fanout,
    )
    e_out[...] = new.reshape(fanout, block, feature)
    summed[pl.ds(here, block), :] = total_of(new, fanout)

    @pl.when(step == steps - 1)
    def _():
        part = 256
        for start in range(0, places, part):
            rows = slice(start, start + part)
            fresh = node_stage(x_ref[rows, :], summed[rows, :])
            number = lax.broadcasted_iota(jnp.int32, (part, mid_places), 0) + start
            lane = lax.broadcasted_iota(jnp.int32, (part, mid_places), 1)
            owner = (number // cols // 4) * (cols // 4) + (number % cols) // 4
            pick = jnp.where(owner == lane, 1.0, 0.0).astype(BF16)
            lifted = dot(dot(pick, mid_new[...]).astype(BF16), prol_ref[...])
            x_out[rows, :] = (fresh.astype(F32) + lifted).astype(BF16)


def per_device(
    fine_nodes, fine_edges, fine_links, mid_nodes, mid_edges, mid_links, coarse_nodes, coarse_edges,
    coarse_links, edge_self, edge_sender, edge_receiver, edge_bias, edge_output, edge_gain, edge_shift,
    node_self, node_summed, node_bias, node_output, node_gain, node_shift, prolongation, pooling,
):
    rows, cols, feature = fine_nodes.shape
    mrows, mcols, _ = mid_nodes.shape
    crows, ccols, _ = coarse_nodes.shape
    fanout = fine_edges.shape[0]
    across, along = lax.axis_size("dx"), lax.axis_size("dy")
    places, mid_places, coarse_places = rows * cols, mrows * mcols, crows * ccols
    stride = cols + 8
    steps = rows // BLOCK
    block = BLOCK * cols
    pad, midpad, pooled = exchange(fine_nodes, mid_nodes)

    whole = lambda shape: pl.BlockSpec(memory_space=pltpu.VMEM)
    operands = [
        fine_links.reshape(fanout * rows, cols),
        mid_links.reshape(fanout * mrows, mcols),
        coarse_links.reshape(fanout * crows, ccols),
        fine_nodes.reshape(places, feature),
        (fine_edges.reshape(fanout, places, feature), pl.BlockSpec((fanout, block, feature), lambda i: (0, i, 0))),
        pad.reshape(-1, feature),
        midpad,
        mid_edges.reshape(fanout * mrows, mcols, feature),
        pooled,
        coarse_nodes.reshape(coarse_places, feature),
        coarse_edges.reshape(fanout * coarse_places, feature),
    ]
    operands += [
        stacked[0] if stacked.ndim == 3 else stacked
        for stacked in (
            edge_self, edge_sender, edge_receiver, edge_bias, edge_output, edge_gain, edge_shift,
            node_self, node_summed, node_bias, node_output, node_gain, node_shift, prolongation, pooling,
        )
    ]
    specs = [item[1] if isinstance(item, tuple) else whole(item.shape) for item in operands]
    values = [item[0] if isinstance(item, tuple) else item for item in operands]
    hidden = edge_self.shape[2]
    struct = lambda *shape: jax.ShapeDtypeStruct(shape, BF16)
    fixed = lambda shape: pl.BlockSpec(shape, lambda i: (0,) * len(shape))
    fine_out, fine_e, mid_out, mid_e, coarse_out, coarse_e = pl.pallas_call(
        functools.partial(update_kernel, fanout, across, along),
        name="update",
        grid=(steps,),
        in_specs=specs,
        out_shape=(
            struct(places, feature),
            struct(fanout, places, feature),
            struct(mrows, mcols, feature),
            struct(fanout * mrows, mcols, feature),
            struct(coarse_places, feature),
            struct(fanout * coarse_places, feature),
        ),
        out_specs=(
            fixed((places, feature)),
            pl.BlockSpec((fanout, block, feature), lambda i: (0, i, 0)),
            fixed((mrows, mcols, feature)),
            fixed((fanout * mrows, mcols, feature)),
            fixed((coarse_places, feature)),
            fixed((fanout * coarse_places, feature)),
        ),
        scratch_shapes=[
            pltpu.VMEM(((rows + 2 * FINE_REACH + 1) * stride, hidden), BF16),
            pltpu.VMEM((places, hidden), F32),
            pltpu.VMEM((fanout * block, hidden), BF16),
            pltpu.VMEM((places, feature), BF16),
            pltpu.VMEM((steps, fanout * BLOCK, cols), F32),
            pltpu.VMEM((fanout * mid_places, feature), F32),
            pltpu.VMEM((mid_places, feature), BF16),
        ],
        compiler_params=pltpu.CompilerParams(vmem_limit_bytes=32 * 1024 * 1024),
    )(*values)
    return (
        fine_out.reshape(fine_nodes.shape),
        fine_e.reshape(fine_edges.shape),
        mid_out.reshape(mid_nodes.shape),
        mid_e.reshape(mid_edges.shape),
        coarse_out.reshape(coarse_nodes.shape),
        coarse_e.reshape(coarse_edges.shape),
    )


def solution(mesh):
    tile = P("dx", "dy", None)
    edge_tile = P(None, "dx", "dy", None)
    link_tile = P(None, "dx", "dy")
    return jax.shard_map(
        per_device,
        mesh=mesh,
        in_specs=(tile, edge_tile, link_tile) * 2 + (P(),) * 18,
        out_specs=(tile, edge_tile, tile, edge_tile, P(), P()),
        check_vma=False,
    )
```
